128 devices in a mesh: req: 8 (over y, core), row: 4 (over z), col: 4 (over x).
Axes of the slice: x: 4, y: 4, z: 4, core: 2. Of those that a mesh axis runs over, the one named last changes fastest.
Arguments:
- tokens: bfloat16 [16384, 1024], P(('req', 'row')), may hold values from -6 to 6
- norm_gain: float32 [1024], replicated, may hold values from 0.5 to 1.5
- w_attn: bfloat16 [5, 1024, 1024], P(None, 'row', 'col'), may hold values from -1 to 1
- persist_kv: bfloat16 [2, 16, 1024], P(None, None, 'col'), may hold values from -6 to 6
- kv_pool: bfloat16 [32, 32, 1, 256, 2, 1024], P(('req', 'row'), None, None, None, None, 'col'), may hold values from -6 to 6
- cache_len: int32 [32], replicated, may hold values from 0 to 8192, as said below
- mem_state: float32 [32, 8, 128, 128], P(('req', 'row'), 'col'), may hold values from -0.5 to 0.5
- decay: float32 [32, 8, 8], P(('req', 'row'), None, 'col'), may hold values from 0.6 to 1
- rate: float32 [32, 8, 8], P(('req', 'row'), None, 'col'), may hold values from 0.05 to 0.5
Outputs:
- mixed: bfloat16 [16384, 1024], P(('req', 'row'), 'col')
- new_state: float32 [32, 8, 128, 128], P(('req', 'row'), 'col')
The draws below stay inside these ranges and needn't reach their ends.
Inputs may be any that keep to these rules, and one draw needn't show every extreme that they name: `cache_len`: cached tokens before each block; some block has exactly 8192.
All inputs are finite; a program needn't handle non-finite values.
Results may differ from the reference program's by a relative error of at most 0.006.
Values may be sent and summed in bfloat16 or wider, within the bound.
A program may use at most 192 MiB of HBM per device.

```python
import math
import jax
import jax.numpy as jnp
from jax import lax

D = 1024
H = 8
HD = 128
NP = 16
S = 512
SEG = 64
PAGE = 256
MAXP = 32
POOL = 32
SPANS = 32
MOST = 1
CACHE = 8192
NSEG = 8


def draw_cache_len(key, part):
    first_key, second_key = jax.random.split(key)
    lengths = jax.random.randint(first_key, (SPANS,), 0, CACHE + 1)
    chosen = jax.random.randint(second_key, (), 0, SPANS)
    return jnp.where(jnp.arange(SPANS) == chosen, CACHE, lengths).astype(jnp.int32)


def clipped_normal(key, shape):
    return jnp.clip(jax.random.normal(key, shape, dtype=jnp.float32), -6.0, 6.0)


def draw_tokens(key, part):
    rows_total = SPANS * S
    values = clipped_normal(jax.random.fold_in(key, 11), (rows_total, D))
    return values.astype(jnp.bfloat16)


def draw_w_attn(key, part):
    values = clipped_normal(jax.random.fold_in(key, 21), (5, D, D)) * D ** (-0.5)
    return values.astype(jnp.bfloat16)


def draw_persist_kv(key, part):
    values = clipped_normal(jax.random.fold_in(key, 31), (2, NP, D))
    return values.astype(jnp.bfloat16)


def draw_kv_pool(key, part):
    values = clipped_normal(jax.random.fold_in(key, 41), (POOL, SPANS, MOST, PAGE, 2, D))
    return values.astype(jnp.bfloat16)


def block_levels(rng, dims, cuts, smallest, high):
    loudness = 1.0
    for position, parts in cuts:
        draws = jax.random.uniform(jax.random.fold_in(jax.random.fold_in(rng, 6), position), (parts,), jnp.float32, smallest / len(cuts), high / len(cuts))
        loudness = loudness * jnp.repeat(jnp.exp(draws), dims[position] // parts).reshape((-1,) + (1,) * (len(dims) - 1 - position))
    return loudness


def bell_draw(own_key, shape, deviation, most, shards=(), held_as=jnp.bfloat16):
    drawn = deviation * jax.random.normal(own_key, shape, jnp.float32)
    if shards:
        drawn = drawn * block_levels(own_key, shape, shards, -0.22, 0.18)
    return jnp.clip(drawn, -most, most).astype(held_as)


def setup_inputs(seed: int = 0) -> dict:
    streams_of = jax.random.split(jax.random.key(seed), 10)
    return {
        "tokens": draw_tokens(jax.random.fold_in(streams_of[9], 71), 0),
        "norm_gain": jnp.clip(1.0 + 0.1 * jax.random.normal(streams_of[1], (D,), jnp.float32), 0.5, 1.5),
        "w_attn": draw_w_attn(jax.random.fold_in(streams_of[9], 71), 0),
        "persist_kv": draw_persist_kv(jax.random.fold_in(streams_of[9], 71), 0),
        "kv_pool": draw_kv_pool(jax.random.fold_in(streams_of[9], 71), 0),
        "cache_len": draw_cache_len(jax.random.fold_in(streams_of[9], 71), 0),
        "mem_state": bell_draw(streams_of[6], (SPANS, H, HD, HD), HD ** -0.5, 0.5, ((0, 32), (1, 4)), jnp.float32),
        "decay": jnp.clip(jnp.exp(math.log(1.0) - 0.5108256 * jax.random.uniform(streams_of[7], (SPANS, NSEG, H), jnp.float32) ** block_levels(streams_of[7], (SPANS, NSEG, H), ((0, 32), (2, 4)), -0.2, 0.2)), 0.6, 1.0),
        "rate": jnp.clip(jnp.exp(math.log(0.5) - 2.3025851 * jax.random.uniform(streams_of[8], (SPANS, NSEG, H), jnp.float32) ** block_levels(streams_of[8], (SPANS, NSEG, H), ((0, 32), (2, 4)), -0.2, 0.2)), 0.05, 0.5),
    }


negative_fill = -1e+30

def reference(tokens, norm_gain, w_attn, persist_kv, kv_pool, cache_len, mem_state, decay, rate):
    xfloat = tokens.astype(jnp.float32)
    normed = (xfloat * lax.rsqrt(lax.optimization_barrier(jnp.mean(xfloat * xfloat, axis=-1, keepdims=True)) + 1e-05) * norm_gain).astype(jnp.bfloat16)
    queries = jnp.dot(normed, w_attn[0], preferred_element_type=jnp.float32).astype(jnp.bfloat16)
    keys_new = jnp.dot(normed, w_attn[1], preferred_element_type=jnp.float32).astype(jnp.bfloat16)
    values_new = jnp.dot(normed, w_attn[2], preferred_element_type=jnp.float32).astype(jnp.bfloat16)
    gate_open = jax.nn.sigmoid(jnp.dot(normed, w_attn[3], preferred_element_type=jnp.float32))
    query_all = queries.reshape(SPANS, S, H, HD)
    keys_all = keys_new.reshape(SPANS, S, H, HD)
    values_all = values_new.reshape(SPANS, S, H, HD)
    persist_keys = persist_kv[0].reshape(NP, H, HD).astype(jnp.float32)
    persist_vals = persist_kv[1].reshape(NP, H, HD).astype(jnp.float32)
    scale_qk = HD ** (-0.5)
    causal = jnp.arange(S, dtype=jnp.int32)[:, None] >= jnp.arange(S, dtype=jnp.int32)[None, :]

    def one_span(span_index):
        device_ids = (span_index + jnp.arange(MAXP, dtype=jnp.int32)) % POOL
        slot_index = jnp.arange(MAXP, dtype=jnp.int32) // POOL
        page_data = kv_pool[device_ids, span_index, slot_index].reshape(CACHE, 2, H, HD).astype(jnp.float32)
        span_query = query_all[span_index].astype(jnp.float32)
        span_keys = keys_all[span_index].astype(jnp.float32)
        span_values = values_all[span_index].astype(jnp.float32)
        keys_cat = jnp.concatenate([persist_keys, page_data[:, 0], span_keys], axis=0)
        vals_cat = jnp.concatenate([persist_vals, page_data[:, 1], span_values], axis=0)
        cache_ok = jnp.arange(CACHE, dtype=jnp.int32) < cache_len[span_index]
        allowed = jnp.concatenate([jnp.ones((S, NP), dtype=bool), jnp.broadcast_to(cache_ok[None, :], (S, CACHE)), causal], axis=1)
        scores = jnp.einsum('shd,khd->hsk', span_query, keys_cat) * scale_qk
        scores = jnp.where(allowed[None], scores, negative_fill)
        maxima = lax.optimization_barrier(jnp.max(scores, axis=-1, keepdims=True))
        probabilities = jnp.where(allowed[None], jnp.exp(scores - maxima), 0.0)
        totals = lax.optimization_barrier(jnp.sum(probabilities, axis=-1))
        rounded = lax.optimization_barrier(probabilities.astype(jnp.bfloat16)).astype(jnp.float32)
        attended = jnp.einsum('hsk,khd->shd', rounded, vals_cat) / jnp.transpose(totals)[:, :, None]
        query_unit = span_query * lax.rsqrt(lax.optimization_barrier(jnp.sum(span_query * span_query, axis=-1, keepdims=True)) + 1e-06)
        key_unit = span_keys * lax.rsqrt(lax.optimization_barrier(jnp.sum(span_keys * span_keys, axis=-1, keepdims=True)) + 1e-06)
        memory = mem_state[span_index]
        span_decay = decay[span_index]
        span_rate = rate[span_index]
        outputs = []
        for segment in range(NSEG):
            lower = segment * SEG
            seg_query = query_unit[lower:lower + SEG]
            seg_keys = key_unit[lower:lower + SEG]
            seg_values = span_values[lower:lower + SEG]
            outputs.append(jnp.einsum('shd,hde->she', seg_query, memory, precision=lax.Precision.HIGHEST))
            errors = jnp.einsum('shd,hde->she', seg_keys, memory, precision=lax.Precision.HIGHEST) - seg_values
            update = jnp.einsum('shd,she->hde', seg_keys, errors, precision=lax.Precision.HIGHEST)
            memory = span_decay[segment][:, None, None] * memory - span_rate[segment][:, None, None] * update
        recalled = jnp.concatenate(outputs, axis=0)
        return (attended, recalled, memory)
    attended, recalled, new_state = lax.map(one_span, jnp.arange(SPANS, dtype=jnp.int32))
    combined = (attended.reshape(SPANS * S, D) + gate_open * recalled.reshape(SPANS * S, D)).astype(jnp.bfloat16)
    mixed = (xfloat + jnp.dot(combined, w_attn[4].T, preferred_element_type=jnp.float32)).astype(jnp.bfloat16)
    return (mixed, new_state)
```

```python
import jax
import jax.numpy as jnp
from jax import lax
from jax.experimental import pallas as pl
from jax.experimental.pallas import tpu as pltpu
from jax.sharding import PartitionSpec as P

HD = 128
NP = 16
SEG = 64
NEG = -1e30
LOG2E = 1.4426950408889634
SCALE = HD ** (-0.5) * LOG2E
F32 = jnp.float32
BF16 = jnp.bfloat16
MESH = pl.DeviceIdType.MESH
HIGH = lax.Precision.HIGHEST
BATCH = 8


def dot(a, b):
    return jnp.dot(a, b, preferred_element_type=F32)


def kernel(
    tok_hbm, gain_ref, w_hbm, persist_hbm, kv_hbm, clen_ref, state_hbm, dr_hbm,
    mixed_ref, newstate_ref,
    tok, normed, wfull, raw, wide, k_own, v_own, k_par, v_par, k_out, v_out,
    qbuf, obuf, sbuf, far_o, far_s, near_o, near_s, loc_o, loc_s,
    keys, vals, valst, gate_t, qun, kun, recall, mem, memt, dr, persist,
    comb, comb_all, w4all, state_in,
    l_sem, p_send, p_recv, w_send, w_recv, kv_send, kv_recv,
    ag_send, ag_recv, rs_send, rs_recv, x4_send, x4_recv, xc_send, xc_recv,
):
    req = lax.axis_index("req")
    z = lax.axis_index("row")
    x = lax.axis_index("col")
    y = req // 2
    k = req % 2
    other = 1 - k

    def at(dx=0, dy=0, dz=0, flip=False):
        core = other if flip else k
        return (((y + dy) % 4) * 2 + core, (z + dz) % 4, (x + dx) % 4)

    def push(src, dst, ssem, rsem, dev):
        copy = pltpu.make_async_remote_copy(
            src_ref=src, dst_ref=dst, send_sem=ssem, recv_sem=rsem,
            device_id=dev, device_id_type=MESH,
        )
        copy.start()
        return copy

    sent = []

    def send(src, dst, ssem, rsem, dev):
        sent.append(push(src, dst, ssem, rsem, dev))

    def arrive(dst, rsem):
        pltpu.make_async_copy(dst, dst, rsem).wait()

    lane = pl.ds(pl.multiple_of(k * HD, HD), HD)
    my_rows = pl.ds(pl.multiple_of(z * 256, 256), 256)
    local = [
        pltpu.make_async_copy(tok_hbm, tok.at[0], l_sem.at[0]),
        pltpu.make_async_copy(w_hbm.at[:, :, lane], wfull.at[:, my_rows, :], l_sem.at[1]),
        pltpu.make_async_copy(persist_hbm.at[:, :, lane], persist, l_sem.at[2]),
        pltpu.make_async_copy(state_hbm.at[k], state_in.at[0], l_sem.at[3]),
        pltpu.make_async_copy(dr_hbm.at[k], dr.at[0], l_sem.at[4]),
    ]
    pages = [
        pltpu.make_async_copy(
            kv_hbm.at[pl.ds(i * BATCH, BATCH)], raw.at[pl.ds(i * BATCH, BATCH)], l_sem.at[5 + i]
        )
        for i in range(4)
    ]
    for c in local:
        c.start()
    for c in pages:
        c.start()

    barrier = pltpu.get_barrier_semaphore()
    peers = [at(flip=True), at(dy=1), at(dy=3), at(dz=1), at(dz=3)]
    for d in (1, 2, 3):
        peers += [at(dx=d), at(dx=d, flip=True)]
    for dev in peers:
        pl.semaphore_signal(barrier, inc=1, device_id=dev, device_id_type=MESH)
    pl.semaphore_wait(barrier, len(peers))

    partner = at(flip=True)
    send(tok_hbm, tok.at[1], p_send.at[0], p_recv.at[0], partner)
    for g, (lo, n) in enumerate(((0, 1), (1, 4))):
        rows = w_hbm.at[pl.ds(lo, n), :, lane]
        land = wfull.at[pl.ds(lo, n), my_rows, :]
        send(rows, land, w_send.at[g, 0], w_recv.at[g, 0], at(dz=1))
        send(rows, land, w_send.at[g, 1], w_recv.at[g, 1], at(dz=3))
    send(state_hbm.at[other], state_in.at[1], p_send.at[1], p_recv.at[1], partner)
    send(dr_hbm.at[other], dr.at[1], p_send.at[2], p_recv.at[2], partner)

    below = pl.multiple_of(((z + 3) % 4) * 256, 256)
    above = pl.multiple_of(((z + 1) % 4) * 256, 256)
    far = pl.multiple_of(((z + 2) % 4) * 256, 256)

    def whole(g, start):
        lo, n = ((0, 1), (1, 4))[g]
        return wfull.at[pl.ds(lo, n), pl.ds(start, 256), :]

    def half(g, start, up):
        if g == 0:
            return wfull.at[pl.ds(0, 1), pl.ds(start + (0 if up else 128), 128), :]
        return wfull.at[pl.ds(1 if up else 3, 2), pl.ds(start, 256), :]

    def weights_forward(g):
        arrive(whole(g, below), w_recv.at[g, 0])
        send(half(g, below, True), half(g, below, True), w_send.at[g, 2], w_recv.at[g, 2], at(dz=1))
        arrive(whole(g, above), w_recv.at[g, 1])
        send(half(g, above, False), half(g, above, False), w_send.at[g, 3], w_recv.at[g, 3], at(dz=3))

    def weights_ready(g):
        arrive(half(g, far, True), w_recv.at[g, 2])
        arrive(half(g, far, False), w_recv.at[g, 3])

    def page(c):
        wide[...] = raw[c].astype(F32)
        k_own[c] = wide[pl.ds(2 * k, 256, stride=4), :].astype(BF16)
        v_own[c] = wide[pl.ds(2 * k + 1, 256, stride=4), :].T.astype(BF16)
        k_out[c] = wide[pl.ds(2 * other, 256, stride=4), :].astype(BF16)
        v_out[c] = wide[pl.ds(2 * other + 1, 256, stride=4), :].T.astype(BF16)

    def page_batch(i):
        pages[i].wait()

        def body(n, carry):
            page(i * BATCH + n)
            return carry

        lax.fori_loop(0, BATCH, body, 0)
        span = pl.ds(i * BATCH, BATCH)
        send(k_out.at[span], k_par.at[span], kv_send.at[i, 0], kv_recv.at[i, 0], partner)
        send(v_out.at[span], v_par.at[span], kv_send.at[i, 1], kv_recv.at[i, 1], partner)

    def norm(j):
        def body(n, carry):
            rows = pl.ds(pl.multiple_of(n * 128, 128), 128)
            v = tok[j, rows, :].astype(F32)
            s = lax.rsqrt(jnp.mean(v * v, axis=-1, keepdims=True) + 1e-05)
            normed[j, rows, :] = (v * s * gain_ref[...]).astype(BF16)
            return carry

        lax.fori_loop(0, 4, body, 0)

    local[0].wait()
    norm(0)
    page_batch(0)
    arrive(tok.at[1], p_recv.at[0])
    norm(1)
    weights_forward(0)
    page_batch(1)
    local[1].wait()
    weights_ready(0)

    def query_body(n, carry):
        j, h = n // 2, n % 2
        rows = pl.ds(pl.multiple_of(h * 256, 256), 256)
        q = dot(normed[j, rows, :], wfull[0])
        qbuf[h, 0, j] = q.T.astype(BF16)
        return carry

    lax.fori_loop(0, 4, query_body, 0)

    def step(h, axis, d):
        along_y = (h == 0) == (axis == 1)
        return at(dy=d) if along_y else at(dz=d)

    def ag_axis1_own():
        for h in (0, 1):
            send(qbuf.at[h, 0], qbuf.at[h, 12], ag_send.at[h, 0, 0], ag_recv.at[h, 12, 0], step(h, 1, 1))
            send(qbuf.at[h, 0], qbuf.at[h, 4], ag_send.at[h, 0, 1], ag_recv.at[h, 4, 0], step(h, 1, 3))

    def ag_axis1_forward():
        for h in (0, 1):
            arrive(qbuf.at[h, 12], ag_recv.at[h, 12, 0])
            send(qbuf.at[h, 12, 0], qbuf.at[h, 8, 0], ag_send.at[h, 12, 2], ag_recv.at[h, 8, 0], step(h, 1, 1))
            arrive(qbuf.at[h, 4], ag_recv.at[h, 4, 0])
            send(qbuf.at[h, 4, 1], qbuf.at[h, 8, 1], ag_send.at[h, 4, 2], ag_recv.at[h, 8, 1], step(h, 1, 3))

    def ag_axis2_own(d1):
        s = d1 * 4
        n = 2 if d1 == 0 else 0
        for h in (0, 1):
            send(qbuf.at[h, s], qbuf.at[h, s + 3], ag_send.at[h, s, n], ag_recv.at[h, s + 3, 0], step(h, 2, 1))
            send(qbuf.at[h, s], qbuf.at[h, s + 1], ag_send.at[h, s, n + 1], ag_recv.at[h, s + 1, 0], step(h, 2, 3))

    def ag_axis2_forward(d1):
        s = d1 * 4
        for h in (0, 1):
            arrive(qbuf.at[h, s + 3], ag_recv.at[h, s + 3, 0])
            send(qbuf.at[h, s + 3, 0], qbuf.at[h, s + 2, 0], ag_send.at[h, s + 3, 2], ag_recv.at[h, s + 2, 0], step(h, 2, 1))
            arrive(qbuf.at[h, s + 1], ag_recv.at[h, s + 1, 0])
            send(qbuf.at[h, s + 1, 1], qbuf.at[h, s + 2, 1], ag_send.at[h, s + 1, 2], ag_recv.at[h, s + 2, 1], step(h, 2, 3))

    def ag_far(s):
        for h in (0, 1):
            for j in (0, 1):
                arrive(qbuf.at[h, s, j], ag_recv.at[h, s, j])

    me = req * 4 + z
    partner_me = (2 * y + other) * 4 + z

    def tasks(count, first, second):
        def body(i, carry):
            n, h, j = i // 4, (i // 2) % 2, i % 2
            d1, d2 = first(n), second(n)
            slot = d1 * 4 + d2
            dy = d1 + h * (d2 - d1)
            dz = d2 + h * (d1 - d2)
            core = k + j * (1 - 2 * k)
            c = (((y + dy) % 4) * 2 + core) * 4 + (z + dz) % 4
            room = clen_ref[c]
            base0 = ((me - c + 32) % 32) * 256
            base1 = ((partner_me - c + 32) % 32) * 256
            q = qbuf[h, slot, j]
            pos = lax.broadcasted_iota(jnp.int32, (256, 256), 0)
            s0 = jnp.where(pos < room - base0, dot(k_own[c], q) * SCALE, NEG)
            s1 = jnp.where(pos < room - base1, dot(k_par[c], q) * SCALE, NEG)
            m = jnp.max(jnp.maximum(s0, s1), axis=0, keepdims=True)
            p0 = jnp.exp2(s0 - m)
            p1 = jnp.exp2(s1 - m)
            total = jnp.sum(p0 + p1, axis=0, keepdims=True)
            out = dot(v_own[c], p0.astype(BF16)) + dot(v_par[c], p1.astype(BF16))
            obuf[h, slot, j] = out.astype(BF16)
            sbuf[h, slot, j, 0:1, :] = m
            sbuf[h, slot, j, 1:2, :] = total
            return carry

        lax.fori_loop(0, 4 * count, body, 0)

    ag_axis1_own()
    ag_axis2_own(0)
    page_batch(2)
    page_batch(3)
    ag_axis1_forward()
    ag_axis2_own(3)
    ag_axis2_own(1)
    for i in range(4):
        span = pl.ds(i * BATCH, BATCH)
        arrive(k_par.at[span], kv_recv.at[i, 0])
        arrive(v_par.at[span], kv_recv.at[i, 1])
    tasks(1, lambda n: 0, lambda n: 0)
    ag_axis2_forward(0)
    ag_far(8)
    ag_axis2_own(2)
    tasks(2, lambda n: 3 - 2 * n, lambda n: 0)
    weights_forward(1)
    ag_axis2_forward(3)
    tasks(2, lambda n: 0, lambda n: 3 - 2 * n)
    ag_axis2_forward(1)
    tasks(1, lambda n: 2, lambda n: 0)
    tasks(2, lambda n: 3, lambda n: 3 - 2 * n)
    ag_axis2_forward(2)
    tasks(2, lambda n: 1, lambda n: 3 - 2 * n)
    ag_far(2)
    tasks(1, lambda n: 0, lambda n: 2)

    def slots(line):
        return (4, 8, 12) if line == 4 else (line * 4 + 1, line * 4 + 2, line * 4 + 3)

    def hop(h, line, d):
        return step(h, 1 if line == 4 else 2, d)

    def rs_far(line):
        s = slots(line)[1]
        for h in (0, 1):
            for j, d in ((0, 1), (1, 3)):
                send(obuf.at[h, s, j], far_o.at[h, line, j], rs_send.at[h, line, j, 0], rs_recv.at[h, line, j, 0], hop(h, line, d))
                send(sbuf.at[h, s, j], far_s.at[h, line, j], rs_send.at[h, line, j, 1], rs_recv.at[h, line, j, 1], hop(h, line, d))

    def merge(pieces):
        m = pieces[0][1][0:1, :]
        for _, st in pieces[1:]:
            m = jnp.maximum(m, st[0:1, :])
        total, out = None, None
        for o, st in pieces:
            f = jnp.exp2(st[0:1, :] - m)
            t = st[1:2, :] * f
            w = o.astype(F32) * f
            total = t if total is None else total + t
            out = w if out is None else out + w
        return out, m, total

    def put(h, slot, j, merged):
        out, m, total = merged
        obuf[h, slot, j] = out.astype(BF16)
        sbuf[h, slot, j, 0:1, :] = m
        sbuf[h, slot, j, 1:2, :] = total

    def rs_near(line):
        for h in (0, 1):
            for j in (0, 1):
                arrive(far_o.at[h, line, j], rs_recv.at[h, line, j, 0])
                arrive(far_s.at[h, line, j], rs_recv.at[h, line, j, 1])
        first, _, last = slots(line)

        def body(i, carry):
            h, j = i // 2, i % 2
            slot = first + j * (last - first)
            put(h, slot, j, merge([(obuf[h, slot, j], sbuf[h, slot, j]), (far_o[h, line, j], far_s[h, line, j])]))
            return carry

        lax.fori_loop(0, 4, body, 0)
        for h in (0, 1):
            for side, (s, d) in enumerate(((first, 1), (last, 3))):
                send(obuf.at[h, s], near_o.at[h, line, side], rs_send.at[h, line, 2 + side, 0], rs_recv.at[h, line, 2 + side, 0], hop(h, line, d))
                send(sbuf.at[h, s], near_s.at[h, line, side], rs_send.at[h, line, 2 + side, 1], rs_recv.at[h, line, 2 + side, 1], hop(h, line, d))

    def near_ready(line):
        for h in (0, 1):
            for side in (0, 1):
                arrive(near_o.at[h, line, side], rs_recv.at[h, line, 2 + side, 0])
                arrive(near_s.at[h, line, side], rs_recv.at[h, line, 2 + side, 1])

    def rs_column(line):
        near_ready(line)

        def body(i, carry):
            h, j = i // 2, i % 2
            slot = line * 4
            put(h, slot, j, merge([
                (obuf[h, slot, j], sbuf[h, slot, j]),
                (near_o[h, line, 0, j], near_s[h, line, 0, j]),
                (near_o[h, line, 1, j], near_s[h, line, 1, j]),
            ]))
            return carry

        lax.fori_loop(0, 4, body, 0)

    rs_far(0)
    tasks(2, lambda n: 2, lambda n: 3 - 2 * n)
    ag_far(14)
    ag_far(6)
    tasks(2, lambda n: 3 - 2 * n, lambda n: 2)
    rs_far(3)
    rs_far(1)
    ag_far(10)
    tasks(1, lambda n: 2, lambda n: 2)
    rs_far(2)

    weights_ready(1)

    def project_body(n, carry):
        j, h = n // 2, n % 2
        rows = pl.ds(pl.multiple_of(h * 256, 256), 256)
        nb = normed[j, rows, :]
        kk = dot(nb, wfull[1]).astype(BF16)
        vv = dot(nb, wfull[2]).astype(BF16)
        keys[j, rows, :] = kk
        vals[j, rows, :] = vv.astype(F32)
        valst[j, h] = vv.astype(F32).T.astype(BF16)
        gate_t[j, h] = jax.nn.sigmoid(dot(nb, wfull[3]).T)
        kf = kk.astype(F32)
        kun[j, rows, :] = kf * lax.rsqrt(jnp.sum(kf * kf, axis=-1, keepdims=True) + 1e-06)
        qf = qbuf[h, 0, j].astype(F32)
        qun[j, h] = qf * lax.rsqrt(jnp.sum(qf * qf, axis=0, keepdims=True) + 1e-06)
        return carry

    lax.fori_loop(0, 4, project_body, 0)

    head = 2 * x + k
    n = 0
    for d in (1, 2, 3):
        cols = pl.ds(pl.multiple_of(((x + d) % 4) * 256, 256), 256)
        for flip in (False, True):
            send(wfull.at[4, cols, :], w4all.at[head], x4_send.at[n], x4_recv.at[d, k], at(dx=d, flip=flip))
            n += 1
    mine = pl.ds(pl.multiple_of(x * 256, 256), 256)
    send(wfull.at[4, mine, :], w4all.at[head], x4_send.at[6], x4_recv.at[0, k], partner)

    rs_near(2)
    local[2].wait()
    w4all[head] = wfull[4, mine, :]

    def own_body(i, carry):
        h, j = i // 2, i % 2
        q = qbuf[h, 0, j]
        token = lax.broadcasted_iota(jnp.int32, (512, 256), 1) + h * 256
        place = lax.broadcasted_iota(jnp.int32, (512, 256), 0)
        s = jnp.where(place <= token, dot(keys[j], q) * SCALE, NEG)
        sp = dot(persist[0], q) * SCALE
        m = jnp.maximum(jnp.max(s, axis=0, keepdims=True), jnp.max(sp, axis=0, keepdims=True))
        p = jnp.exp2(s - m)
        pp = jnp.exp2(sp - m)
        total = jnp.sum(p, axis=0, keepdims=True) + jnp.sum(pp, axis=0, keepdims=True)
        pb = p.astype(BF16)
        out = dot(valst[j, 0], pb[:256]) + dot(valst[j, 1], pb[256:])
        out = out + lax.dot_general(persist[1], pp.astype(BF16), (((0,), (0,)), ((), ())), preferred_element_type=F32)
        loc_o[h, j] = out
        loc_s[h, j, 0:1, :] = m
        loc_s[h, j, 1:2, :] = total
        return carry

    lax.fori_loop(0, 4, own_body, 0)

    rs_near(3)
    rs_near(1)

    local[3].wait()
    local[4].wait()
    arrive(state_in.at[1], p_recv.at[1])
    arrive(dr.at[1], p_recv.at[2])
    for j in (0, 1):
        memt[j] = state_in[j].T

    def memory_body(t, carry):
        lanes = lax.broadcasted_iota(jnp.int32, (HD, HD), 1)
        for j in (0, 1):
            h, lo = t // 2, pl.multiple_of((t % 2) * HD, HD)
            q = qun[j, h, :, pl.ds(lo, HD)]
            parts = []
            for u in (0, 1):
                seg = 2 * t + u
                rows = pl.ds(pl.multiple_of(seg * SEG, SEG), SEG)
                kn = kun[j, rows, :]
                vs = vals[j, rows, :]
                m_now = memt[j]
                parts.append(jnp.dot(m_now, q, precision=HIGH, preferred_element_type=F32))
                gram = lax.dot_general(kn, kn, (((0,), (0,)), ((), ())), precision=HIGH, preferred_element_type=F32)
                target = lax.dot_general(vs, kn, (((0,), (0,)), ((), ())), precision=HIGH, preferred_element_type=F32)
                update = jnp.dot(m_now, gram, precision=HIGH, preferred_element_type=F32) - target
                memt[j] = dr[j, pl.ds(seg, 1), :] * m_now - dr[j, pl.ds(8 + seg, 1), :] * update
            recall[j, h, :, pl.ds(lo, HD)] = jnp.where(lanes < SEG, parts[0], parts[1])
        return carry

    lax.fori_loop(0, 4, memory_body, 0)
    for j in (0, 1):
        mem[j] = memt[j].T
    send(mem.at[1], state_in.at[2], p_send.at[3], p_recv.at[3], partner)

    rs_near(0)
    rs_column(2)
    rs_far(4)
    rs_column(3)
    rs_column(1)
    rs_near(4)
    near_ready(0)
    near_ready(4)

    def final_body(i, carry):
        h, j = i // 2, i % 2
        out, _, total = merge([
            (obuf[h, 0, j], sbuf[h, 0, j]),
            (near_o[h, 0, 0, j], near_s[h, 0, 0, j]),
            (near_o[h, 0, 1, j], near_s[h, 0, 1, j]),
            (near_o[h, 4, 0, j], near_s[h, 4, 0, j]),
            (near_o[h, 4, 1, j], near_s[h, 4, 1, j]),
            (loc_o[h, j], loc_s[h, j]),
        ])
        comb[h, j] = (out / total + gate_t[j, h] * recall[j, h]).astype(BF16)
        return carry

    lax.fori_loop(0, 4, final_body, 0)

    def slot_of(d, core):
        return ((x + d) % 4) * 2 + core

    for h in (0, 1):
        for n, (dx, flip) in enumerate(((1, False), (1, True), (3, False), (3, True), (0, True))):
            j = 1 if flip else 0
            send(comb.at[h, j], comb_all.at[h, head], xc_send.at[h, n], xc_recv.at[h, (4 - dx) % 4, k], at(dx=dx, flip=flip))
    for h in (0, 1):
        comb_all[h, head] = comb[h, 0]
    for h in (0, 1):
        for core in (0, 1):
            arrive(comb_all.at[h, slot_of(3, core)], xc_recv.at[h, 3, core])
            arrive(comb_all.at[h, slot_of(1, core)], xc_recv.at[h, 1, core])
        up, down = slot_of(3, 0), slot_of(1, 1)
        send(comb_all.at[h, up], comb_all.at[h, up], xc_send.at[h, 5], xc_recv.at[h, 2, 0], at(dx=1))
        send(comb_all.at[h, down], comb_all.at[h, down], xc_send.at[h, 6], xc_recv.at[h, 2, 1], at(dx=3))
    for d in (1, 2, 3):
        for core in (0, 1):
            arrive(w4all.at[slot_of(4 - d, core)], x4_recv.at[d, core])
    arrive(w4all.at[slot_of(0, other)], x4_recv.at[0, other])

    arrive(state_in.at[2], p_recv.at[3])
    newstate_ref[k] = mem[0]
    newstate_ref[other] = state_in[2]

    for h in (0, 1):
        arrive(comb_all.at[h, slot_of(0, other)], xc_recv.at[h, 0, other])
        for core in (0, 1):
            arrive(comb_all.at[h, slot_of(2, core)], xc_recv.at[h, 2, core])
        acc = dot(w4all[0], comb_all[h, 0])
        for g in range(1, 8):
            acc = acc + dot(w4all[g], comb_all[h, g])
        rows = pl.ds(h * 256, 256)
        resid = tok[0, rows, pl.ds(pl.multiple_of(x * 256, 256), 256)].astype(F32)
        mixed_ref[rows, :] = (resid + acc.T).astype(BF16)

    for c in sent:
        c.wait_send()


def shards(tokens, norm_gain, w_attn, persist_kv, kv_pool, cache_len, mem_state, decay, rate):
    kv = kv_pool.reshape(32, 256, 2, 2, HD).transpose(0, 1, 3, 2, 4).reshape(32, 1024, HD)
    dr = jnp.concatenate([decay[0], rate[0]], axis=0).T
    dr = jnp.broadcast_to(dr[:, :, None], (2, 16, HD))
    hbm = pl.BlockSpec(memory_space=pl.ANY)
    vmem = pl.BlockSpec(memory_space=pltpu.VMEM)
    V = pltpu.VMEM
    dma = pltpu.SemaphoreType.DMA
    mixed, new_state = pl.pallas_call(
        kernel,
        out_shape=(
            jax.ShapeDtypeStruct((512, 256), BF16),
            jax.ShapeDtypeStruct((2, HD, HD), F32),
        ),
        in_specs=[hbm, vmem, hbm, hbm, hbm, pl.BlockSpec(memory_space=pltpu.SMEM), hbm, hbm],
        out_specs=(vmem, vmem),
        scratch_shapes=[
            V((2, 512, 1024), BF16),
            V((2, 512, 1024), BF16),
            V((5, 1024, HD), BF16),
            V((32, 1024, HD), BF16),
            V((1024, HD), F32),
            V((32, 256, HD), BF16), V((32, HD, 256), BF16),
            V((32, 256, HD), BF16), V((32, HD, 256), BF16),
            V((32, 256, HD), BF16), V((32, HD, 256), BF16),
            V((2, 16, 2, HD, 256), BF16),
            V((2, 16, 2, HD, 256), BF16),
            V((2, 16, 2, 2, 256), F32),
            V((2, 5, 2, HD, 256), BF16), V((2, 5, 2, 2, 256), F32),
            V((2, 5, 2, 2, HD, 256), BF16), V((2, 5, 2, 2, 2, 256), F32),
            V((2, 2, HD, 256), F32), V((2, 2, 2, 256), F32),
            V((2, 512, HD), BF16), V((2, 512, HD), F32), V((2, 2, HD, 256), BF16),
            V((2, 2, HD, 256), F32), V((2, 2, HD, 256), F32), V((2, 512, HD), F32),
            V((2, 2, HD, 256), F32),
            V((2, HD, HD), F32), V((2, HD, HD), F32),
            V((2, 16, HD), F32), V((2, NP, HD), BF16),
            V((2, 2, HD, 256), BF16), V((2, 8, HD, 256), BF16),
            V((8, 256, HD), BF16),
            V((3, HD, HD), F32),
            dma((9,)), dma((4,)), dma((4,)), dma((2, 4)), dma((2, 4)), dma((4, 2)), dma((4, 2)),
            dma((2, 16, 4)), dma((2, 16, 2)), dma((2, 5, 4, 2)), dma((2, 5, 4, 2)),
            dma((7,)), dma((4, 2)), dma((2, 7)), dma((2, 4, 2)),
        ],
        compiler_params=pltpu.CompilerParams(
            collective_id=0, has_side_effects=True, vmem_limit_bytes=60 * 1024 * 1024
        ),
        name="prefill",
    )(tokens, norm_gain[None], w_attn, persist_kv, kv, cache_len, mem_state[0], dr)
    return (mixed, new_state[None])


def solution(mesh):
    return jax.shard_map(
        shards,
        mesh=mesh,
        in_specs=(
            P(("req", "row"), None),
            P(),
            P(None, "row", "col"),
            P(None, None, "col"),
            P(("req", "row"), None, None, None, None, "col"),
            P(),
            P(("req", "row"), "col", None, None),
            P(("req", "row"), None, "col"),
            P(("req", "row"), None, "col"),
        ),
        out_specs=(P(("req", "row"), "col"), P(("req", "row"), "col", None, None)),
        check_vma=False,
    )
```

```python
import jax
import jax.numpy as jnp
from jax import lax
from jax.experimental import pallas as pl
from jax.experimental.pallas import tpu as pltpu
from jax.sharding import PartitionSpec as P

HD = 128
NP = 16
SEG = 64
NEG = -1e30
LOG2E = 1.4426950408889634
SCALE = HD ** (-0.5) * LOG2E
F32 = jnp.float32
BF16 = jnp.bfloat16
MESH = pl.DeviceIdType.MESH
HIGH = lax.Precision.HIGHEST
BATCH = 8
GROUPS = ((0, 1), (1, 3), (4, 1))
VR = HD + 16


def dot(a, b):
    return jnp.dot(a, b, preferred_element_type=F32)


def kernel(
    tok_hbm, gain_ref, w_hbm, persist_hbm, kv_hbm, clen_ref, state_hbm, decay_ref, rate_ref,
    mixed_ref, newstate_ref,
    tok, normed, wfull, raw, wide, k_own, v_own, k_par, v_par, k_out, v_out, bias,
    qbuf, obuf, sbuf, far_o, far_s, near_o, near_s, loc_o, loc_s,
    keys, vals, valst, gate_t, qun, kun, recall, mem, memt, dr, dr_out, persist,
    comb, comb_all, w4all, state_in,
    l_sem, p_send, p_recv, w_send, w_recv, kv_send, kv_recv,
    ag_send, ag_recv, rs_send, rs_recv, x4_send, x4_recv, xc_send, xc_recv,
):
    req = lax.axis_index("req")
    z = lax.axis_index("row")
    x = lax.axis_index("col")
    y = req // 2
    k = req % 2
    other = 1 - k

    def at(dx=0, dy=0, dz=0, flip=False):
        core = other if flip else k
        return (((y + dy) % 4) * 2 + core, (z + dz) % 4, (x + dx) % 4)

    def push(src, dst, ssem, rsem, dev):
        copy = pltpu.make_async_remote_copy(
            src_ref=src, dst_ref=dst, send_sem=ssem, recv_sem=rsem,
            device_id=dev, device_id_type=MESH,
        )
        copy.start()
        return copy

    sent = []

    def send(src, dst, ssem, rsem, dev):
        sent.append(push(src, dst, ssem, rsem, dev))

    def arrive(dst, rsem):
        pltpu.make_async_copy(dst, dst, rsem).wait()

    lane = pl.ds(pl.multiple_of(k * HD, HD), HD)
    my_rows = pl.ds(pl.multiple_of(z * 256, 256), 256)
    local = [
        pltpu.make_async_copy(tok_hbm, tok.at[0], l_sem.at[0]),
        pltpu.make_async_copy(w_hbm.at[:, :, lane], wfull.at[:, my_rows, :], l_sem.at[1]),
        pltpu.make_async_copy(persist_hbm.at[:, :, lane], persist, l_sem.at[2]),
        pltpu.make_async_copy(state_hbm.at[k], state_in.at[0], l_sem.at[3]),
    ]
    pages = [
        pltpu.make_async_copy(
            kv_hbm.at[pl.ds(i * BATCH, BATCH)], raw.at[pl.ds(i * BATCH, BATCH)], l_sem.at[5 + i]
        )
        for i in range(4)
    ]
    for c in local:
        c.start()
    for c in pages:
        c.start()

    barrier = pltpu.get_barrier_semaphore()
    peers = [at(flip=True), at(dy=1), at(dy=3), at(dz=1), at(dz=3)]
    for d in (1, 2, 3):
        peers += [at(dx=d), at(dx=d, flip=True)]
    for dev in peers:
        pl.semaphore_signal(barrier, inc=1, device_id=dev, device_id_type=MESH)
    pl.semaphore_wait(barrier, len(peers))

    def weights_own(g):
        lo, n = GROUPS[g]
        rows = w_hbm.at[pl.ds(lo, n), :, lane]
        land = wfull.at[pl.ds(lo, n), my_rows, :]
        send(rows, land, w_send.at[g, 0], w_recv.at[g, 0], at(dz=1))
        send(rows, land, w_send.at[g, 1], w_recv.at[g, 1], at(dz=3))

    partner = at(flip=True)
    weights_own(0)
    send(tok_hbm, tok.at[1], p_send.at[0], p_recv.at[0], partner)
    send(state_hbm.at[other], state_in.at[1], p_send.at[1], p_recv.at[1], partner)
    for n in range(8):
        for hh in (0, 1):
            dr_out[hh, n : n + 1, :] = jnp.full((1, HD), decay_ref[hh, n], F32)
            dr_out[hh, 8 + n : 9 + n, :] = jnp.full((1, HD), rate_ref[hh, n], F32)
    send(dr_out.at[other], dr.at[1], p_send.at[2], p_recv.at[2], partner)
    dr[0] = dr_out[k]

    below = pl.multiple_of(((z + 3) % 4) * 256, 256)
    above = pl.multiple_of(((z + 1) % 4) * 256, 256)
    far = pl.multiple_of(((z + 2) % 4) * 256, 256)

    def whole(g, start):
        lo, n = GROUPS[g]
        return wfull.at[pl.ds(lo, n), pl.ds(start, 256), :]

    def half(g, start, up):
        lo, n = GROUPS[g]
        return wfull.at[pl.ds(lo, n), pl.ds(start + (0 if up else 128), 128), :]

    def weights_forward(g):
        arrive(whole(g, below), w_recv.at[g, 0])
        send(half(g, below, True), half(g, below, True), w_send.at[g, 2], w_recv.at[g, 2], at(dz=1))
        arrive(whole(g, above), w_recv.at[g, 1])
        send(half(g, above, False), half(g, above, False), w_send.at[g, 3], w_recv.at[g, 3], at(dz=3))

    def weights_ready(g):
        arrive(half(g, far, True), w_recv.at[g, 2])
        arrive(half(g, far, False), w_recv.at[g, 3])

    me = req * 4 + z
    partner_me = (2 * y + other) * 4 + z

    def page(c):
        place = lax.broadcasted_iota(jnp.int32, (256, HD), 0)
        for i, pool in ((0, me), (1, partner_me)):
            room = clen_ref[c] - ((pool - c + 32) % 32) * 256
            bias[c, i] = jnp.where(place < room, 0.0, NEG)
        v_own[c, HD:, :] = jnp.ones((16, 256), BF16)
        v_par[c, HD:, :] = jnp.ones((16, 256), BF16)
        wide[...] = raw[c].astype(F32)
        k_own[c] = wide[pl.ds(2 * k, 256, stride=4), :].astype(BF16)
        v_own[c, :HD, :] = wide[pl.ds(2 * k + 1, 256, stride=4), :].T.astype(BF16)
        k_out[c] = wide[pl.ds(2 * other, 256, stride=4), :].astype(BF16)
        v_out[c] = wide[pl.ds(2 * other + 1, 256, stride=4), :].T.astype(BF16)

    def page_batch(i):
        pages[i].wait()

        def body(n, carry):
            page(i * BATCH + n)
            return carry

        lax.fori_loop(0, BATCH, body, 0)
        span = pl.ds(i * BATCH, BATCH)
        send(k_out.at[span], k_par.at[span], kv_send.at[i, 0], kv_recv.at[i, 0], partner)
        send(v_out.at[span], v_par.at[span, pl.ds(0, HD)], kv_send.at[i, 1], kv_recv.at[i, 1], partner)

    def norm(j):
        def body(n, carry):
            rows = pl.ds(pl.multiple_of(n * 128, 128), 128)
            v = tok[j, rows, :].astype(F32)
            s = lax.rsqrt(jnp.mean(v * v, axis=-1, keepdims=True) + 1e-05)
            normed[j, rows, :] = (v * s * gain_ref[...]).astype(BF16)
            return carry

        lax.fori_loop(0, 4, body, 0)

    local[0].wait()
    norm(0)
    page_batch(0)
    arrive(tok.at[1], p_recv.at[0])
    norm(1)
    weights_forward(0)
    weights_own(1)
    page_batch(1)
    local[1].wait()
    weights_ready(0)

    def query_body(n, carry):
        j, h = n // 2, n % 2
        rows = pl.ds(pl.multiple_of(h * 256, 256), 256)
        q = dot(normed[j, rows, :], wfull[0])
        qbuf[h, 0, j] = q.T.astype(BF16)
        return carry

    lax.fori_loop(0, 4, query_body, 0)

    def step(h, axis, d):
        along_y = (h == 0) == (axis == 1)
        return at(dy=d) if along_y else at(dz=d)

    def ag_axis1_own():
        for h in (0, 1):
            send(qbuf.at[h, 0], qbuf.at[h, 12], ag_send.at[h, 0, 0], ag_recv.at[h, 12, 0], step(h, 1, 1))
            send(qbuf.at[h, 0], qbuf.at[h, 4], ag_send.at[h, 0, 1], ag_recv.at[h, 4, 0], step(h, 1, 3))

    def ag_axis1_forward():
        for h in (0, 1):
            arrive(qbuf.at[h, 12], ag_recv.at[h, 12, 0])
            send(qbuf.at[h, 12, 0], qbuf.at[h, 8, 0], ag_send.at[h, 12, 2], ag_recv.at[h, 8, 0], step(h, 1, 1))
            arrive(qbuf.at[h, 4], ag_recv.at[h, 4, 0])
            send(qbuf.at[h, 4, 1], qbuf.at[h, 8, 1], ag_send.at[h, 4, 2], ag_recv.at[h, 8, 1], step(h, 1, 3))

    def ag_axis2_own(d1):
        s = d1 * 4
        n = 2 if d1 == 0 else 0
        for h in (0, 1):
            send(qbuf.at[h, s], qbuf.at[h, s + 3], ag_send.at[h, s, n], ag_recv.at[h, s + 3, 0], step(h, 2, 1))
            send(qbuf.at[h, s], qbuf.at[h, s + 1], ag_send.at[h, s, n + 1], ag_recv.at[h, s + 1, 0], step(h, 2, 3))

    def ag_axis2_forward(d1):
        s = d1 * 4
        for h in (0, 1):
            arrive(qbuf.at[h, s + 3], ag_recv.at[h, s + 3, 0])
            send(qbuf.at[h, s + 3, 0], qbuf.at[h, s + 2, 0], ag_send.at[h, s + 3, 2], ag_recv.at[h, s + 2, 0], step(h, 2, 1))
            arrive(qbuf.at[h, s + 1], ag_recv.at[h, s + 1, 0])
            send(qbuf.at[h, s + 1, 1], qbuf.at[h, s + 2, 1], ag_send.at[h, s + 1, 2], ag_recv.at[h, s + 2, 1], step(h, 2, 3))

    def ag_far(s):
        for h in (0, 1):
            for j in (0, 1):
                arrive(qbuf.at[h, s, j], ag_recv.at[h, s, j])

    def tasks(count, first, second):
        def body(i, carry):
            n, h = i // 2, i % 2
            d1, d2 = first(n), second(n)
            slot = d1 * 4 + d2
            dy = d1 + h * (d2 - d1)
            dz = d2 + h * (d1 - d2)
            blocks = [(((y + dy) % 4) * 2 + core) * 4 + (z + dz) % 4 for core in (k, other)]
            scores = []
            for j, c in enumerate(blocks):
                q = qbuf[h, slot, j]
                mask = [jnp.concatenate([bias[c, i]] * 2, axis=1) for i in (0, 1)]
                scores.append((dot(k_own[c], q) + mask[0], dot(k_par[c], q) + mask[1]))
            for j, c in enumerate(blocks):
                s0, s1 = scores[j]
                m = jnp.max(jnp.maximum(s0, s1), axis=0, keepdims=True)
                p0 = jnp.exp2((s0 - m) * SCALE).astype(BF16)
                p1 = jnp.exp2((s1 - m) * SCALE).astype(BF16)
                out = dot(v_own[c], p0) + dot(v_par[c], p1)
                obuf[h, slot, j] = out[:HD].astype(BF16)
                sbuf[h, slot, j, 0:1, :] = m * SCALE
                sbuf[h, slot, j, 1:2, :] = out[HD : HD + 1]
            return carry

        lax.fori_loop(0, 2 * count, body, 0)

    ag_axis1_own()
    ag_axis2_own(0)
    page_batch(2)
    page_batch(3)
    ag_axis1_forward()
    ag_axis2_own(3)
    for i in range(4):
        span = pl.ds(i * BATCH, BATCH)
        arrive(k_par.at[span], kv_recv.at[i, 0])
        arrive(v_par.at[span, pl.ds(0, HD)], kv_recv.at[i, 1])
    tasks(1, lambda n: 0, lambda n: 0)
    ag_far(8)
    ag_axis2_own(2)
    ag_axis2_own(1)
    weights_forward(1)
    weights_own(2)
    tasks(2, lambda n: 3 - 2 * n, lambda n: 0)
    ag_axis2_forward(0)
    tasks(2, lambda n: 0, lambda n: 3 - 2 * n)
    ag_axis2_forward(3)
    tasks(1, lambda n: 2, lambda n: 0)
    ag_axis2_forward(2)
    tasks(2, lambda n: 3, lambda n: 3 - 2 * n)
    ag_axis2_forward(1)
    weights_forward(2)
    tasks(2, lambda n: 2, lambda n: 3 - 2 * n)
    ag_far(2)
    tasks(1, lambda n: 0, lambda n: 2)

    def slots(line):
        return (4, 8, 12) if line == 4 else (line * 4 + 1, line * 4 + 2, line * 4 + 3)

    def hop(h, line, d):
        return step(h, 1 if line == 4 else 2, d)

    def rs_far(line):
        s = slots(line)[1]
        for h in (0, 1):
            for j, d in ((0, 1), (1, 3)):
                send(obuf.at[h, s, j], far_o.at[h, line, j], rs_send.at[h, line, j, 0], rs_recv.at[h, line, j, 0], hop(h, line, d))
                send(sbuf.at[h, s, j], far_s.at[h, line, j], rs_send.at[h, line, j, 1], rs_recv.at[h, line, j, 1], hop(h, line, d))

    def merge(pieces):
        m = pieces[0][1][0:1, :]
        for _, st in pieces[1:]:
            m = jnp.maximum(m, st[0:1, :])
        total, out = None, None
        for o, st in pieces:
            f = jnp.exp2(st[0:1, :] - m)
            t = st[1:2, :] * f
            w = o.astype(F32) * f
            total = t if total is None else total + t
            out = w if out is None else out + w
        return out, m, total

    def put(h, slot, j, merged):
        out, m, total = merged
        obuf[h, slot, j] = out.astype(BF16)
        sbuf[h, slot, j, 0:1, :] = m
        sbuf[h, slot, j, 1:2, :] = total

    def rs_near(line):
        for h in (0, 1):
            for j in (0, 1):
                arrive(far_o.at[h, line, j], rs_recv.at[h, line, j, 0])
                arrive(far_s.at[h, line, j], rs_recv.at[h, line, j, 1])
        first, _, last = slots(line)

        def body(i, carry):
            h, j = i // 2, i % 2
            slot = first + j * (last - first)
            put(h, slot, j, merge([(obuf[h, slot, j], sbuf[h, slot, j]), (far_o[h, line, j], far_s[h, line, j])]))
            return carry

        lax.fori_loop(0, 4, body, 0)
        for h in (0, 1):
            for side, (s, d) in enumerate(((first, 1), (last, 3))):
                send(obuf.at[h, s], near_o.at[h, line, side], rs_send.at[h, line, 2 + side, 0], rs_recv.at[h, line, 2 + side, 0], hop(h, line, d))
                send(sbuf.at[h, s], near_s.at[h, line, side], rs_send.at[h, line, 2 + side, 1], rs_recv.at[h, line, 2 + side, 1], hop(h, line, d))

    def near_ready(line):
        for h in (0, 1):
            for side in (0, 1):
                arrive(near_o.at[h, line, side], rs_recv.at[h, line, 2 + side, 0])
                arrive(near_s.at[h, line, side], rs_recv.at[h, line, 2 + side, 1])

    def rs_column(line):
        near_ready(line)

        def body(i, carry):
            h, j = i // 2, i % 2
            slot = line * 4
            put(h, slot, j, merge([
                (obuf[h, slot, j], sbuf[h, slot, j]),
                (near_o[h, line, 0, j], near_s[h, line, 0, j]),
                (near_o[h, line, 1, j], near_s[h, line, 1, j]),
            ]))
            return carry

        lax.fori_loop(0, 4, body, 0)

    rs_far(0)
    ag_far(10)
    tasks(1, lambda n: 2, lambda n: 2)
    rs_far(2)
    tasks(2, lambda n: 1, lambda n: 3 - 2 * n)
    ag_far(14)
    ag_far(6)
    tasks(2, lambda n: 3 - 2 * n, lambda n: 2)
    rs_far(3)
    rs_far(1)
    rs_near(2)

    weights_ready(1)

    def project_body(n, carry):
        j, h = n // 2, n % 2
        rows = pl.ds(pl.multiple_of(h * 256, 256), 256)
        nb = normed[j, rows, :]
        kk = dot(nb, wfull[1]).astype(BF16)
        vv = dot(nb, wfull[2]).astype(BF16)
        keys[j, rows, :] = kk
        vals[j, rows, :] = vv.astype(F32)
        valst[j, h] = vv.astype(F32).T.astype(BF16)
        gate_t[j, h] = jax.nn.sigmoid(dot(nb, wfull[3]).T)
        kf = kk.astype(F32)
        kun[j, rows, :] = kf * lax.rsqrt(jnp.sum(kf * kf, axis=-1, keepdims=True) + 1e-06)
        qf = qbuf[h, 0, j].astype(F32)
        qun[j, h] = qf * lax.rsqrt(jnp.sum(qf * qf, axis=0, keepdims=True) + 1e-06)
        return carry

    lax.fori_loop(0, 4, project_body, 0)
    rs_near(3)
    rs_near(1)
    weights_ready(2)

    head = 2 * x + k
    n = 0
    for d in (1, 2, 3):
        cols = pl.ds(pl.multiple_of(((x + d) % 4) * 256, 256), 256)
        for flip in (False, True):
            send(wfull.at[4, cols, :], w4all.at[head], x4_send.at[n], x4_recv.at[d, k], at(dx=d, flip=flip))
            n += 1
    mine = pl.ds(pl.multiple_of(x * 256, 256), 256)
    send(wfull.at[4, mine, :], w4all.at[head], x4_send.at[6], x4_recv.at[0, k], partner)

    local[2].wait()
    w4all[head] = wfull[4, mine, :]

    def own_body(i, carry):
        h, j = i // 2, i % 2
        q = qbuf[h, 0, j]
        token = lax.broadcasted_iota(jnp.int32, (512, 256), 1) + h * 256
        place = lax.broadcasted_iota(jnp.int32, (512, 256), 0)
        s = jnp.where(place <= token, dot(keys[j], q) * SCALE, NEG)
        sp = dot(persist[0], q) * SCALE
        m = jnp.maximum(jnp.max(s, axis=0, keepdims=True), jnp.max(sp, axis=0, keepdims=True))
        p = jnp.exp2(s - m)
        pp = jnp.exp2(sp - m)
        total = jnp.sum(p, axis=0, keepdims=True) + jnp.sum(pp, axis=0, keepdims=True)
        pb = p.astype(BF16)
        out = dot(valst[j, 0], pb[:256]) + dot(valst[j, 1], pb[256:])
        out = out + lax.dot_general(persist[1], pp.astype(BF16), (((0,), (0,)), ((), ())), preferred_element_type=F32)
        loc_o[h, j] = out
        loc_s[h, j, 0:1, :] = m
        loc_s[h, j, 1:2, :] = total
        return carry

    lax.fori_loop(0, 4, own_body, 0)

    rs_column(2)
    rs_far(4)
    rs_near(0)

    local[3].wait()
    arrive(state_in.at[1], p_recv.at[1])
    arrive(dr.at[1], p_recv.at[2])
    for j in (0, 1):
        memt[j] = state_in[j].T

    def memory_body(t, carry):
        lanes = lax.broadcasted_iota(jnp.int32, (HD, HD), 1)
        for j in (0, 1):
            h, lo = t // 2, pl.multiple_of((t % 2) * HD, HD)
            q = qun[j, h, :, pl.ds(lo, HD)]
            parts = []
            for u in (0, 1):
                seg = 2 * t + u
                rows = pl.ds(pl.multiple_of(seg * SEG, SEG), SEG)
                kn = kun[j, rows, :]
                vs = vals[j, rows, :]
                m_now = memt[j]
                parts.append(jnp.dot(m_now, q, precision=HIGH, preferred_element_type=F32))
                gram = lax.dot_general(kn, kn, (((0,), (0,)), ((), ())), precision=HIGH, preferred_element_type=F32)
                target = lax.dot_general(vs, kn, (((0,), (0,)), ((), ())), precision=HIGH, preferred_element_type=F32)
                update = jnp.dot(m_now, gram, precision=HIGH, preferred_element_type=F32) - target
                memt[j] = dr[j, pl.ds(seg, 1), :] * m_now - dr[j, pl.ds(8 + seg, 1), :] * update
            recall[j, h, :, pl.ds(lo, HD)] = jnp.where(lanes < SEG, parts[0], parts[1])
        return carry

    lax.fori_loop(0, 4, memory_body, 0)
    for j in (0, 1):
        mem[j] = memt[j].T
    send(mem.at[1], state_in.at[2], p_send.at[3], p_recv.at[3], partner)

    rs_column(3)
    rs_column(1)
    rs_near(4)
    near_ready(0)
    near_ready(4)

    def final_body(i, carry):
        h, j = i // 2, i % 2
        out, _, total = merge([
            (obuf[h, 0, j], sbuf[h, 0, j]),
            (near_o[h, 0, 0, j], near_s[h, 0, 0, j]),
            (near_o[h, 0, 1, j], near_s[h, 0, 1, j]),
            (near_o[h, 4, 0, j], near_s[h, 4, 0, j]),
            (near_o[h, 4, 1, j], near_s[h, 4, 1, j]),
            (loc_o[h, j], loc_s[h, j]),
        ])
        comb[h, j] = (out / total + gate_t[j, h] * recall[j, h]).astype(BF16)
        return carry

    lax.fori_loop(0, 4, final_body, 0)

    def slot_of(d, core):
        return ((x + d) % 4) * 2 + core

    for h in (0, 1):
        for n, (dx, flip) in enumerate(((1, False), (1, True), (3, False), (3, True), (0, True))):
            j = 1 if flip else 0
            send(comb.at[h, j], comb_all.at[h, head], xc_send.at[h, n], xc_recv.at[h, (4 - dx) % 4, k], at(dx=dx, flip=flip))
    for h in (0, 1):
        comb_all[h, head] = comb[h, 0]
    for h in (0, 1):
        for core in (0, 1):
            arrive(comb_all.at[h, slot_of(3, core)], xc_recv.at[h, 3, core])
            arrive(comb_all.at[h, slot_of(1, core)], xc_recv.at[h, 1, core])
        up, down = slot_of(3, 0), slot_of(1, 1)
        send(comb_all.at[h, up], comb_all.at[h, up], xc_send.at[h, 5], xc_recv.at[h, 2, 0], at(dx=1))
        send(comb_all.at[h, down], comb_all.at[h, down], xc_send.at[h, 6], xc_recv.at[h, 2, 1], at(dx=3))
    for d in (1, 2, 3):
        for core in (0, 1):
            arrive(w4all.at[slot_of(4 - d, core)], x4_recv.at[d, core])
    arrive(w4all.at[slot_of(0, other)], x4_recv.at[0, other])

    arrive(state_in.at[2], p_recv.at[3])
    newstate_ref[k] = mem[0]
    newstate_ref[other] = state_in[2]

    for h in (0, 1):
        arrive(comb_all.at[h, slot_of(0, other)], xc_recv.at[h, 0, other])
        for core in (0, 1):
            arrive(comb_all.at[h, slot_of(2, core)], xc_recv.at[h, 2, core])
        acc = dot(w4all[0], comb_all[h, 0])
        for g in range(1, 8):
            acc = acc + dot(w4all[g], comb_all[h, g])
        rows = pl.ds(h * 256, 256)
        resid = tok[0, rows, pl.ds(pl.multiple_of(x * 256, 256), 256)].astype(F32)
        mixed_ref[rows, :] = (resid + acc.T).astype(BF16)

    for c in sent:
        c.wait_send()


def shards(tokens, norm_gain, w_attn, persist_kv, kv_pool, cache_len, mem_state, decay, rate):
    kv = kv_pool.reshape(32, 256, 2, 2, HD).transpose(0, 1, 3, 2, 4).reshape(32, 1024, HD)
    hbm = pl.BlockSpec(memory_space=pl.ANY)
    vmem = pl.BlockSpec(memory_space=pltpu.VMEM)
    smem = pl.BlockSpec(memory_space=pltpu.SMEM)
    V = pltpu.VMEM
    dma = pltpu.SemaphoreType.DMA
    mixed, new_state = pl.pallas_call(
        kernel,
        out_shape=(
            jax.ShapeDtypeStruct((512, 256), BF16),
            jax.ShapeDtypeStruct((2, HD, HD), F32),
        ),
        in_specs=[hbm, vmem, hbm, hbm, hbm, smem, hbm, smem, smem],
        out_specs=(vmem, vmem),
        scratch_shapes=[
            V((2, 512, 1024), BF16),
            V((2, 512, 1024), BF16),
            V((5, 1024, HD), BF16),
            V((32, 1024, HD), BF16),
            V((1024, HD), F32),
            V((32, 256, HD), BF16), V((32, VR, 256), BF16),
            V((32, 256, HD), BF16), V((32, VR, 256), BF16),
            V((32, 256, HD), BF16), V((32, HD, 256), BF16),
            V((32, 2, 256, HD), F32),
            V((2, 16, 2, HD, 256), BF16),
            V((2, 16, 2, HD, 256), BF16),
            V((2, 16, 2, 2, 256), F32),
            V((2, 5, 2, HD, 256), BF16), V((2, 5, 2, 2, 256), F32),
            V((2, 5, 2, 2, HD, 256), BF16), V((2, 5, 2, 2, 2, 256), F32),
            V((2, 2, HD, 256), F32), V((2, 2, 2, 256), F32),
            V((2, 512, HD), BF16), V((2, 512, HD), F32), V((2, 2, HD, 256), BF16),
            V((2, 2, HD, 256), F32), V((2, 2, HD, 256), F32), V((2, 512, HD), F32),
            V((2, 2, HD, 256), F32),
            V((2, HD, HD), F32), V((2, HD, HD), F32),
            V((2, 16, HD), F32), V((2, 16, HD), F32), V((2, NP, HD), BF16),
            V((2, 2, HD, 256), BF16), V((2, 8, HD, 256), BF16),
            V((8, 256, HD), BF16),
            V((3, HD, HD), F32),
            dma((9,)), dma((4,)), dma((4,)), dma((3, 4)), dma((3, 4)), dma((4, 2)), dma((4, 2)),
            dma((2, 16, 4)), dma((2, 16, 2)), dma((2, 5, 4, 2)), dma((2, 5, 4, 2)),
            dma((7,)), dma((4, 2)), dma((2, 7)), dma((2, 4, 2)),
        ],
        compiler_params=pltpu.CompilerParams(
            collective_id=0, has_side_effects=True, vmem_limit_bytes=60 * 1024 * 1024
        ),
        name="prefill",
    )(tokens, norm_gain[None], w_attn, persist_kv, kv, cache_len, mem_state[0], decay[0].T, rate[0].T)
    return (mixed, new_state[None])


def solution(mesh):
    return jax.shard_map(
        shards,
        mesh=mesh,
        in_specs=(
            P(("req", "row"), None),
            P(),
            P(None, "row", "col"),
            P(None, None, "col"),
            P(("req", "row"), None, None, None, None, "col"),
            P(),
            P(("req", "row"), "col", None, None),
            P(("req", "row"), None, "col"),
            P(("req", "row"), None, "col"),
        ),
        out_specs=(P(("req", "row"), "col"), P(("req", "row"), "col", None, None)),
        check_vma=False,
    )
```
